32 devices in a mesh: row: 2 (over x), col: 16 (over z, y, core).
Axes of the slice: x: 2, y: 2, z: 4, core: 2. Of those that a mesh axis runs over, the one named last changes fastest.
Arguments:
- coords: float32 [64, 3, 256], P(('row', 'col')), may hold values from 0 to 8, as said below
- noise_var: float32 [64, 256], P(('row', 'col')), may hold values from 0.1 to 1
- right_side: float32 [64, 8, 256], P(('row', 'col')), may hold values from -32 to 32
- start_guess: float32 [64, 8, 256], P(('row', 'col')), may hold values from -3 to 3
- tile_pairs: int32 [2, 16, 2, 63], P('row', 'col'), may hold values from -1 to 31, as said below
Outputs:
- solution_field: float32 [64, 8, 256], P(('row', 'col'))
- residual: float32 [64, 8, 256], P(('row', 'col'))
The draws below stay inside these ranges and needn't reach their ends.
Inputs may be any that keep to these rules, and one draw needn't show every extreme that they name: `coords`: each tile's points lie within one unit cell of the integer lattice, and distinct tiles lie in distinct cells. `tile_pairs`: each device's list holds every pair of its block whose cells differ by at most one in each coordinate, each pair once and no other; listed entries come first, then entries of -1 in both rows.
All inputs are finite; a program needn't handle non-finite values.
Results may differ from the reference program's by a relative error of at most 0.0003.
Values sent between devices are 32-bit elements; how exact they have to be, the bound alone decides.
A program may use at most 64 MiB of HBM per device.

```python
import math
import jax
import jax.numpy as jnp
from jax import lax

TILE = 256
TPP = 2
RHS = 8
ITERS = 3
TILES = 64
TMAX = 63
N_ROW = 2
N_COL = 16


def lattice_cells(key):
    key_x, key_y = jax.random.split(jax.random.fold_in(key, 7))
    offset_row = jax.random.randint(key_x, (), 0, N_ROW)
    offset_col = jax.random.randint(key_y, (), 0, N_COL)
    tiles = jnp.arange(TILES, dtype=jnp.int32)
    pieces = tiles // TPP
    within = tiles % TPP
    row_index = pieces // N_COL
    col_index = pieces % N_COL
    half_rows = N_ROW // 2
    shifted_row = (row_index + offset_row) % N_ROW
    box_x = shifted_row // half_rows
    box_y = shifted_row % half_rows
    depth = N_COL // 8
    half_cols = N_COL // 2
    place = (col_index + offset_col) % N_COL
    local_x = place // half_cols
    step = place % half_cols
    local_y = step // depth
    lane = step % depth
    local_z = jnp.where(local_y % 2 == 0, lane, depth - 1 - lane)
    local_x = local_x + 2 * within
    local_y = (local_y + 2 * within) % 4
    local_z = (local_z + depth // 2 * within) % depth
    cell_x = 4 * box_x + local_x
    cell_y = 4 * box_y + local_y
    return jnp.stack([cell_x, cell_y, local_z], axis=1).astype(jnp.int32)


def draw_coords(key, part):
    cells = lattice_cells(key)
    fraction = jax.random.uniform(jax.random.fold_in(key, 11), (TILES, 3, TILE), jnp.float32)
    return cells[:, :, None].astype(jnp.float32) + fraction


def draw_tile_pairs(key, part):
    cells = lattice_cells(key)
    row_block = TPP * N_COL
    col_block = TPP * N_ROW
    row_ids = jnp.arange(N_ROW, dtype=jnp.int32)[:, None] * row_block + jnp.arange(row_block, dtype=jnp.int32)[None, :]
    col_local = jnp.arange(col_block, dtype=jnp.int32)[None, :]
    col_ids = (col_local // TPP * N_COL + jnp.arange(N_COL, dtype=jnp.int32)[:, None]) * TPP + col_local % TPP
    row_cells = cells[row_ids]
    col_cells = cells[col_ids]
    spacing = jnp.abs(row_cells[:, None, :, None, :] - col_cells[None, :, None, :, :])
    touching = jnp.all(spacing <= 1, axis=-1).astype(jnp.int32)
    flat = touching.reshape(N_ROW, N_COL, row_block * col_block)
    scores = jax.random.permutation(jax.random.fold_in(key, 13), row_block * col_block).astype(jnp.int32)
    ranking = (1 - flat) * (row_block * col_block) + scores[None, None, :]
    sorted_index = jnp.argsort(ranking, axis=-1, stable=True)[:, :, :TMAX].astype(jnp.int32)
    listed = jnp.take_along_axis(flat, sorted_index, axis=-1)
    row_tiles = jnp.where(listed > 0, sorted_index // col_block, -1)
    col_tiles = jnp.where(listed > 0, sorted_index % col_block, -1)
    return jnp.stack([row_tiles, col_tiles], axis=2).astype(jnp.int32)


def draw_right_side(key, part):
    key_values = jax.random.fold_in(jax.random.fold_in(key, 17), 0)
    key_column = jax.random.fold_in(jax.random.fold_in(key, 17), 2)
    position = jnp.arange(TILES, dtype=jnp.float32) / (TILES - 1)
    column_scale = 0.5 * 4.0 ** jax.random.uniform(key_column, (RHS,), jnp.float32)
    point_scale = 0.4 * 10.0 ** position
    values = jnp.clip(jax.random.normal(key_values, (TILES, RHS, TILE), jnp.float32), -4.0, 4.0)
    return values * point_scale[:, None, None] * column_scale[None, :, None]


def levels(rng, dims, cuts, low, top_value):
    factor_of = 1.0
    for dim, parts in cuts:
        heights = jax.random.uniform(jax.random.fold_in(jax.random.fold_in(rng, 6), dim), (parts,), jnp.float32, low / len(cuts), top_value / len(cuts))
        factor_of = factor_of * jnp.repeat(jnp.exp(heights), dims[dim] // parts).reshape((-1,) + (1,) * (len(dims) - 1 - dim))
    return factor_of


def normal_values(stream_key, extent, spread, bound, cuts=(), held_as=jnp.bfloat16):
    gain = levels(stream_key, extent, cuts, -0.22, 0.18) if cuts else 1.0
    result = jax.random.normal(stream_key, extent, jnp.float32) * spread * gain
    return jnp.minimum(jnp.maximum(result, -bound), bound).astype(held_as)


def setup_inputs(seed: int = 0) -> dict:
    streams_of = jax.random.split(jax.random.key(seed), 6)
    coords = draw_coords(jax.random.fold_in(streams_of[5], 71), 0)
    noise_var = jnp.clip(jnp.exp(math.log(1.0) - 2.3025851 * jax.random.uniform(streams_of[1], (TILES, TILE), jnp.float32) ** levels(streams_of[1], (TILES, TILE), ((0, 32),), -0.2, 0.2)), 0.1, 1.0)
    right_side = draw_right_side(jax.random.fold_in(streams_of[5], 71), 0)
    start_guess = normal_values(streams_of[3], (TILES, RHS, TILE), 0.5, 3.0, ((0, 32),), jnp.float32)
    tile_pairs = draw_tile_pairs(jax.random.fold_in(streams_of[5], 71), 0)
    return {"coords": coords, "noise_var": noise_var, "right_side": right_side, "start_guess": start_guess, "tile_pairs": tile_pairs}


def wendland(left_points, right_points):
    squared = jnp.zeros((left_points.shape[0], left_points.shape[2], right_points.shape[2]), jnp.float32)
    for component in range(3):
        spacing = left_points[:, component, :, None] - right_points[:, component, None, :]
        squared = squared + spacing * spacing
    distance = jnp.sqrt(squared)
    remain = jnp.maximum(1.0 - distance, 0.0)
    return remain ** 4 * (4.0 * distance + 1.0)

def global_pairs(tile_pairs):
    rows_local = tile_pairs[:, :, 0, :]
    cols_local = tile_pairs[:, :, 1, :]
    usable = rows_local >= 0
    row_grid = jnp.arange(N_ROW, dtype=jnp.int32)[:, None, None]
    col_grid = jnp.arange(N_COL, dtype=jnp.int32)[None, :, None]
    row_tiles = row_grid * (TPP * N_COL) + jnp.maximum(rows_local, 0)
    safe_cols = jnp.maximum(cols_local, 0)
    col_tiles = (safe_cols // TPP * N_COL + col_grid) * TPP + safe_cols % TPP
    total_pairs = N_ROW * N_COL * TMAX
    extra = -total_pairs % 64
    row_tiles = jnp.pad(row_tiles.reshape(-1), (0, extra)).astype(jnp.int32).reshape(-1, 64)
    col_tiles = jnp.pad(col_tiles.reshape(-1), (0, extra)).astype(jnp.int32).reshape(-1, 64)
    usable = jnp.pad(usable.reshape(-1), (0, extra)).reshape(-1, 64)
    return (row_tiles, col_tiles, usable)

def apply_operator(vectors, coords, noise_var, pairs):

    def accumulate(totals, group):
        rows_group, cols_group, use_group = group
        weights = wendland(coords[rows_group], coords[cols_group]) * use_group[:, None, None].astype(jnp.float32)
        product = jnp.einsum('pab,psb->psa', weights, vectors[cols_group], precision=lax.Precision.HIGHEST)
        return (totals.at[rows_group].add(product), None)
    totals, ignored = lax.scan(accumulate, jnp.zeros_like(vectors), pairs)
    return totals + noise_var[:, None, :] * vectors

def reference(coords, noise_var, right_side, start_guess, tile_pairs):
    pairs = global_pairs(tile_pairs)
    solution_field = start_guess
    residual = right_side - apply_operator(start_guess, coords, noise_var, pairs)
    direction = residual
    norm_now = lax.optimization_barrier(jnp.sum(residual * residual, axis=(0, 2)))
    for iteration in range(ITERS):
        applied = apply_operator(direction, coords, noise_var, pairs)
        step_size = norm_now / lax.optimization_barrier(jnp.sum(direction * applied, axis=(0, 2)))
        solution_field = solution_field + step_size[None, :, None] * direction
        residual = residual - step_size[None, :, None] * applied
        norm_next = lax.optimization_barrier(jnp.sum(residual * residual, axis=(0, 2)))
        direction = residual + (norm_next / norm_now)[None, :, None] * direction
        norm_now = norm_next
    return (solution_field, residual)
```

```python
import functools

import jax
import jax.numpy as jnp
from jax import lax
from jax.experimental import pallas as pl
from jax.experimental.pallas import tpu as pltpu
from jax.sharding import PartitionSpec as P

ITERS = 3
GROUP = 4
NEAR = 27
CAPACITY = -(-NEAR // GROUP) * GROUP
CORES = 2
MESH = pl.DeviceIdType.MESH
VMEM_SPEC = pl.BlockSpec(memory_space=pltpu.VMEM)
SMEM_SPEC = pl.BlockSpec(memory_space=pltpu.SMEM)
ANY_SPEC = pl.BlockSpec(memory_space=pl.ANY)


def factors(mesh_shape):
    rows, cols = mesh_shape
    chips = cols // CORES
    wide = 1
    while wide * wide * 4 <= chips:
        wide *= 2
    return rows, chips // wide, wide, CORES


def gather_kernel(dims, count, *refs):
    xs, zs, ys, cs = dims
    ins, outs = refs[:count], refs[count : 2 * count]
    send_sem, recv_sem, local_sem = refs[2 * count :]
    x = lax.axis_index("row")
    col = lax.axis_index("col")
    z, y, c = col // (ys * cs), (col // cs) % ys, col % cs

    def device(xx, zz, yy, cc):
        return (xx, (zz * ys + yy) * cs + cc)

    def slot(xx, zz, yy, cc):
        return ((xx * zs + zz) * ys + yy) * cs + cc

    balanced = xs == 2 and ys == 2
    partners = [device(x, (z + k) % zs, y, c) for k in range(1, zs)]
    partners += [device(x, z, (y + k) % ys, c) for k in range(1, ys)]
    partners += [device((x + k) % xs, z, y, c) for k in range(1, xs)]
    partners += [device(x, z, y, 1 - c)]
    barrier = pltpu.get_barrier_semaphore()
    for partner in partners:
        pl.semaphore_signal(barrier, inc=1, device_id=partner, device_id_type=MESH)
    local = []
    for a in range(count):
        copy = pltpu.make_async_copy(ins[a], outs[a].at[slot(x, z, y, c)], local_sem.at[a])
        copy.start()
        local.append(copy)
    pl.semaphore_wait(barrier, len(partners))

    numbers = iter(range(10**6))
    sent = []

    def send(a, source, place, target):
        number = next(numbers)
        copy = pltpu.make_async_remote_copy(
            src_ref=source,
            dst_ref=outs[a].at[place],
            send_sem=send_sem.at[number],
            recv_sem=recv_sem.at[number],
            device_id=target,
            device_id_type=MESH,
        )
        copy.start()
        sent.append(copy)
        return copy

    mine = slot(x, z, y, c)
    other = device(x, z, y, 1 - c)
    along_z = {}
    for k in range(1, zs):
        for a in range(count):
            along_z[k, a] = send(a, ins[a], mine, device(x, (z + k) % zs, y, c))
    for a in range(count):
        local[a].wait()

    if xs == 2 and ys == 2:
        x2, y2 = (x + c) % 2, (y + 1 - c) % 2
        x3, y3 = (x + 1 - c) % 2, (y + c) % 2
        ahead, aside, late, swaps = {}, {}, {}, []
        steps = [(k, a) for k in range(zs) for a in range(count)]
        for k, a in steps:
            if k:
                along_z[k, a].wait_recv()
            place = slot(x, (z - k + zs) % zs, y, c)
            ahead[k, a] = send(a, outs[a].at[place], place, device(x2, z, y2, c))
            aside[k, a] = send(a, outs[a].at[place], place, device(x3, z, y3, c))
            swaps.append(send(a, outs[a].at[place], place, other))
        for k, a in steps:
            ahead[k, a].wait_recv()
            place = slot(x2, (z - k + zs) % zs, y2, c)
            late[k, a] = send(a, outs[a].at[place], place, device(x3, z, y3, c))
            swaps.append(send(a, outs[a].at[place], place, other))
        for k, a in steps:
            aside[k, a].wait_recv()
            place = slot(x3, (z - k + zs) % zs, y3, c)
            swaps.append(send(a, outs[a].at[place], place, other))
        for k, a in steps:
            late[k, a].wait_recv()
            place = slot(1 - x, (z - k + zs) % zs, 1 - y, c)
            swaps.append(send(a, outs[a].at[place], place, other))
        for copy in swaps:
            copy.wait_recv()
        for copy in sent:
            copy.wait_send()
        return

    def across(places, targets):
        for place in places:
            for a in range(count):
                for target in targets:
                    send(a, outs[a].at[place], place, target)

    def settle():
        for copy in sent:
            copy.wait()
        del sent[:]

    settle()
    across(
        [slot(x, zz, y, c) for zz in range(zs)],
        [device(x, z, (y + k) % ys, c) for k in range(1, ys)],
    )
    settle()
    across(
        [slot(x, zz, yy, c) for zz in range(zs) for yy in range(ys)],
        [device((x + k) % xs, z, y, c) for k in range(1, xs)],
    )
    settle()
    across(
        [slot(xx, zz, yy, c) for xx in range(xs) for zz in range(zs) for yy in range(ys)],
        [other],
    )
    settle()


def all_gather(dims, collective_id, *slabs):
    xs, zs, ys, cs = dims
    devices = xs * zs * ys * cs
    count = len(slabs)
    copies = count * (devices - 1)
    return pl.pallas_call(
        functools.partial(gather_kernel, dims, count),
        out_shape=[jax.ShapeDtypeStruct((devices,) + s.shape, s.dtype) for s in slabs],
        in_specs=[VMEM_SPEC] * count,
        out_specs=[VMEM_SPEC] * count,
        scratch_shapes=[
            pltpu.SemaphoreType.DMA((copies,)),
            pltpu.SemaphoreType.DMA((copies,)),
            pltpu.SemaphoreType.DMA((count,)),
        ],
        compiler_params=pltpu.CompilerParams(collective_id=collective_id, has_side_effects=True),
    )(*slabs)


def split_rows(values):
    high = values.astype(jnp.bfloat16)
    low = (values - high.astype(jnp.float32)).astype(jnp.bfloat16)
    return jnp.concatenate([high, low], axis=0)


def product(near_ref, groups, vectors_ref, blocks, place, tile, wait):
    depth = 2 * tile * GROUP

    def step(g, total):
        wait(g)
        parts = []
        for i in range(GROUP):
            part = vectors_ref[near_ref[place, g * GROUP + i]]
            parts += [part, part]
        first = pl.multiple_of((place * (CAPACITY // GROUP) + g) * depth, depth)
        return total + jnp.dot(
            jnp.concatenate(parts, axis=1),
            blocks[pl.ds(first, depth), :],
            preferred_element_type=jnp.float32,
        )

    rhs2 = vectors_ref.shape[1]
    total = lax.fori_loop(0, groups, step, jnp.zeros((rhs2, tile), jnp.float32))
    return total[: rhs2 // 2] + total[rhs2 // 2 :]


def block_copy(blocks, blocks_hbm, sems, place, g, depth, out):
    number = place * (CAPACITY // GROUP) + g
    part = pl.ds(pl.multiple_of(number * depth, depth), depth)
    if out:
        return pltpu.make_async_copy(blocks.at[part, :], blocks_hbm.at[part, :], sems.at[number])
    return pltpu.make_async_copy(blocks_hbm.at[part, :], blocks.at[part, :], sems.at[number])


def build_kernel(
    flags_ref, points_ref, own_ref, guess_ref, own_guess_ref, side_ref, noise_ref,
    residual_ref, blocks_hbm, near_ref, count_ref, blocks, vectors_ref, sems,
):
    tiles, tile = points_ref.shape[0], points_ref.shape[2]
    own = own_ref.shape[0]
    depth = 2 * tile * GROUP
    rows = 32

    def split_one(t, carry):
        vectors_ref[t] = split_rows(guess_ref[t])
        return carry

    lax.fori_loop(0, tiles, split_one, 0, unroll=4)
    for place in range(own):
        def listing(t, number):
            near_ref[place, number] = t
            return number + flags_ref[place, t]

        number = lax.fori_loop(0, tiles, listing, jnp.int32(0))
        for i in range(GROUP):
            near_ref[place, number + i] = 0
        groups = (number + GROUP - 1) // GROUP
        count_ref[place] = groups
        right = own_ref[place]
        base = place * CAPACITY * 2 * tile

        def one(e, carry):
            left = points_ref[near_ref[place, e]].T
            start = base + e * (2 * tile)
            for chunk in range(tile // rows):
                squared = None
                for component in range(3):
                    spacing = (
                        left[chunk * rows : (chunk + 1) * rows, component : component + 1]
                        - right[component : component + 1, :]
                    )
                    term = spacing * spacing
                    squared = term if squared is None else squared + term
                distance = jnp.sqrt(squared)
                remain = jnp.maximum(1.0 - distance, 0.0)
                remain = remain * remain
                weights = remain * remain * (4.0 * distance + 1.0)
                high = weights.astype(jnp.bfloat16)
                low = (weights - high.astype(jnp.float32)).astype(jnp.bfloat16)
                at = pl.multiple_of(start + chunk * rows, rows)
                blocks[pl.ds(at, rows), :] = high
                at = pl.multiple_of(start + tile + chunk * rows, rows)
                blocks[pl.ds(at, rows), :] = low
            return carry

        def empty(e, carry):
            at = pl.multiple_of(base + e * (2 * tile), 2 * tile)
            blocks[pl.ds(at, 2 * tile), :] = jnp.zeros((2 * tile, tile), jnp.bfloat16)
            return carry

        lax.fori_loop(0, number, one, 0)
        lax.fori_loop(number, groups * GROUP, empty, 0)

        def start_out(g, carry):
            block_copy(blocks, blocks_hbm, sems, place, g, depth, True).start()
            return carry

        lax.fori_loop(0, groups, start_out, 0)
        image = product(near_ref, groups, vectors_ref, blocks, place, tile, lambda g: None)
        image = image + noise_ref[place : place + 1, :] * own_guess_ref[place]
        residual_ref[place] = side_ref[place] - image
    for place in range(own):
        def wait_out(g, carry):
            block_copy(blocks, blocks_hbm, sems, place, g, depth, True).wait()
            return carry

        lax.fori_loop(0, count_ref[place], wait_out, 0)


def step_kernel(first, *refs):
    refs = list(refs)
    near_ref, count_ref, me_ref, noise_ref, blocks_hbm = refs[:5]
    refs = refs[5:]
    if first:
        (res_ref, field_ref), refs = refs[:2], refs[2:]
    else:
        (image_ref, res_ref, dir_ref, norm_ref, field_ref), refs = refs[:5], refs[5:]
    (out_image, out_res, out_dir, out_norm, out_field, out_dot), refs = refs[:6], refs[6:]
    blocks, vectors_ref, sems = refs
    tiles, rhs, tile = res_ref.shape
    own = noise_ref.shape[0]
    depth = 2 * tile * GROUP
    me = me_ref[0]
    for place in range(own):
        def start_in(g, carry):
            block_copy(blocks, blocks_hbm, sems, place, g, depth, False).start()
            return carry

        lax.fori_loop(0, count_ref[place], start_in, 0)
    zero = jnp.zeros((rhs, tile), jnp.float32)
    if first:
        def square(t, total):
            value = res_ref[t]
            vectors_ref[t] = split_rows(value)
            out_dir[t] = value
            out_res[t] = value
            return total + value * value

        norm = jnp.sum(lax.fori_loop(0, tiles, square, zero, unroll=4), axis=1, keepdims=True)
        out_field[...] = field_ref[...]
    else:
        def dots(t, total):
            return total + dir_ref[t] * image_ref[t]

        norm_old = norm_ref[:, :1]
        inner = jnp.sum(lax.fori_loop(0, tiles, dots, zero, unroll=4), axis=1, keepdims=True)
        step_size = norm_old / inner
        for place in range(own):
            out_field[place] = field_ref[place] + step_size * dir_ref[me * own + place]

        def descend(t, total):
            value = res_ref[t] - step_size * image_ref[t]
            out_res[t] = value
            return total + value * value

        norm = jnp.sum(lax.fori_loop(0, tiles, descend, zero, unroll=4), axis=1, keepdims=True)
        turn = norm / norm_old

        def redirect(t, carry):
            value = out_res[t] + turn * dir_ref[t]
            out_dir[t] = value
            vectors_ref[t] = split_rows(value)
            return carry

        lax.fori_loop(0, tiles, redirect, 0, unroll=4)
    out_norm[...] = jnp.broadcast_to(norm, out_norm.shape)
    total = zero
    for place in range(own):
        groups = count_ref[place]

        def wait(g):
            block_copy(blocks, blocks_hbm, sems, place, g, depth, False).wait()

        image = product(near_ref, groups, vectors_ref, blocks, place, tile, wait)
        value = out_dir[me * own + place]
        image = image + noise_ref[place : place + 1, :] * value
        out_image[place] = image
        total = total + value * image
    out_dot[...] = jnp.broadcast_to(jnp.sum(total, axis=1, keepdims=True), out_dot.shape)


def shards(mesh_shape, coords, noise_var, right_side, start_guess, tile_pairs):
    dims = factors(mesh_shape)
    devices = mesh_shape[0] * mesh_shape[1]
    own, _, tile = coords.shape
    rhs = right_side.shape[1]
    tiles = own * devices
    me = (lax.axis_index("row") * mesh_shape[1] + lax.axis_index("col")).astype(jnp.int32)
    padded = jnp.pad(coords, ((0, 0), (0, 5), (0, 0)))
    points, guess = all_gather(dims, 0, padded, start_guess)
    points = points.reshape(tiles, 8, tile)
    guess = guess.reshape(tiles, rhs, tile)
    low, high = jnp.min(points, axis=2), jnp.max(points, axis=2)
    own_low, own_high = jnp.min(padded, axis=2), jnp.max(padded, axis=2)
    gap = jnp.maximum(low[None] - own_high[:, None], own_low[:, None] - high[None])
    flags = jnp.all(gap < 1.0, axis=2).astype(jnp.int32)

    f32 = jnp.float32
    full = jax.ShapeDtypeStruct((tiles, rhs, tile), f32)
    slab = jax.ShapeDtypeStruct((own, rhs, tile), f32)
    small = jax.ShapeDtypeStruct((rhs, 128), f32)
    block_shape = (own * CAPACITY * 2 * tile, tile)
    scratch = [
        pltpu.VMEM(block_shape, jnp.bfloat16),
        pltpu.VMEM((tiles, 2 * rhs, tile), jnp.bfloat16),
        pltpu.SemaphoreType.DMA((own * CAPACITY // GROUP,)),
    ]
    params = pltpu.CompilerParams(vmem_limit_bytes=56 * 2**20)
    residual, blocks, near, count = pl.pallas_call(
        build_kernel,
        out_shape=[
            slab,
            jax.ShapeDtypeStruct(block_shape, jnp.bfloat16),
            jax.ShapeDtypeStruct((own, CAPACITY + GROUP), jnp.int32),
            jax.ShapeDtypeStruct((own,), jnp.int32),
        ],
        in_specs=[SMEM_SPEC] + [VMEM_SPEC] * 6,
        out_specs=[VMEM_SPEC, ANY_SPEC, SMEM_SPEC, SMEM_SPEC],
        scratch_shapes=scratch,
        compiler_params=params,
    )(flags, points, padded, guess, start_guess, right_side, noise_var)

    def advance(first, operands):
        return pl.pallas_call(
            functools.partial(step_kernel, first),
            out_shape=[slab, full, full, small, slab, small],
            in_specs=[SMEM_SPEC] * 3 + [VMEM_SPEC, ANY_SPEC] + [VMEM_SPEC] * len(operands),
            out_specs=[VMEM_SPEC] * 6,
            scratch_shapes=scratch,
            compiler_params=params,
        )(near, count, me[None], noise_var, blocks, *operands)

    (gathered,) = all_gather(dims, 1, residual)
    image, residual, direction, norm, field, dot = advance(
        True, (gathered.reshape(full.shape), start_guess)
    )
    for iteration in range(1, ITERS):
        (gathered,) = all_gather(dims, 1 + iteration, image)
        image, residual, direction, norm, field, dot = advance(
            False, (gathered.reshape(full.shape), residual, direction, norm, field)
        )
    (dots,) = all_gather(dims, 1 + ITERS, dot)
    step_size = (norm[:, :1] / jnp.sum(dots[:, :, :1], axis=0))[None]
    own_res = lax.dynamic_slice_in_dim(residual, me * own, own)
    own_dir = lax.dynamic_slice_in_dim(direction, me * own, own)
    return field + step_size * own_dir, own_res - step_size * image


def solution(mesh):
    placed = (
        P(("row", "col"), None, None),
        P(("row", "col"), None),
        P(("row", "col"), None, None),
        P(("row", "col"), None, None),
        P("row", "col", None, None),
    )
    return jax.shard_map(
        functools.partial(shards, (mesh.shape["row"], mesh.shape["col"])),
        mesh=mesh,
        in_specs=placed,
        out_specs=(P(("row", "col"), None, None), P(("row", "col"), None, None)),
        check_vma=False,
    )
```

```python
import functools

import jax
import jax.numpy as jnp
from jax import lax
from jax.experimental import pallas as pl
from jax.experimental.pallas import tpu as pltpu
from jax.sharding import PartitionSpec as P

ITERS = 3
GROUP = 4
NEAR = 27
CAPACITY = -(-NEAR // GROUP) * GROUP
CORES = 2
MESH = pl.DeviceIdType.MESH
VMEM_SPEC = pl.BlockSpec(memory_space=pltpu.VMEM)
SMEM_SPEC = pl.BlockSpec(memory_space=pltpu.SMEM)
ANY_SPEC = pl.BlockSpec(memory_space=pl.ANY)


def factors(mesh_shape):
    rows, cols = mesh_shape
    chips = cols // CORES
    wide = 1
    while wide * wide * 4 <= chips:
        wide *= 2
    return rows, chips // wide, wide, CORES


def position(dims):
    xs, zs, ys, cs = dims
    x = lax.axis_index("row")
    col = lax.axis_index("col")
    return x, col // (ys * cs), (col // cs) % ys, col % cs


def gather_partners(dims):
    xs, zs, ys, cs = dims
    x, z, y, c = position(dims)
    partners = [(x, (((z + k) % zs) * ys + y) * cs + c) for k in range(1, zs)]
    partners += [(x, (z * ys + (y + k) % ys) * cs + c) for k in range(1, ys)]
    partners += [((x + k) % xs, (z * ys + y) * cs + c) for k in range(1, xs)]
    partners += [(x, (z * ys + y) * cs + 1 - c)]
    return partners


def gather(dims, ins, outs, send_sem, recv_sem, local_sem):
    xs, zs, ys, cs = dims
    count = len(ins)
    x, z, y, c = position(dims)

    def device(xx, zz, yy, cc):
        return (xx, (zz * ys + yy) * cs + cc)

    def slot(xx, zz, yy, cc):
        return ((xx * zs + zz) * ys + yy) * cs + cc

    local = []
    for a in range(count):
        copy = pltpu.make_async_copy(ins[a], outs[a].at[slot(x, z, y, c)], local_sem.at[a])
        copy.start()
        local.append(copy)

    numbers = iter(range(10**6))
    sent = []

    def send(a, source, place, target):
        number = next(numbers)
        copy = pltpu.make_async_remote_copy(
            src_ref=source,
            dst_ref=outs[a].at[place],
            send_sem=send_sem.at[number],
            recv_sem=recv_sem.at[number],
            device_id=target,
            device_id_type=MESH,
        )
        copy.start()
        sent.append(copy)
        return copy

    mine = slot(x, z, y, c)
    other = device(x, z, y, 1 - c)
    along_z = {}
    for k in range(1, zs):
        for a in range(count):
            along_z[k, a] = send(a, ins[a], mine, device(x, (z + k) % zs, y, c))
    for a in range(count):
        local[a].wait()

    if xs == 2 and ys == 2:
        x2, y2 = (x + c) % 2, (y + 1 - c) % 2
        x3, y3 = (x + 1 - c) % 2, (y + c) % 2
        ahead, aside, late, swaps = {}, {}, {}, []
        steps = [(k, a) for k in range(zs) for a in range(count)]
        for k, a in steps:
            if k:
                along_z[k, a].wait_recv()
            place = slot(x, (z - k + zs) % zs, y, c)
            ahead[k, a] = send(a, outs[a].at[place], place, device(x2, z, y2, c))
            aside[k, a] = send(a, outs[a].at[place], place, device(x3, z, y3, c))
            swaps.append(send(a, outs[a].at[place], place, other))
        for k, a in steps:
            ahead[k, a].wait_recv()
            place = slot(x2, (z - k + zs) % zs, y2, c)
            late[k, a] = send(a, outs[a].at[place], place, device(x3, z, y3, c))
            swaps.append(send(a, outs[a].at[place], place, other))
        for k, a in steps:
            aside[k, a].wait_recv()
            place = slot(x3, (z - k + zs) % zs, y3, c)
            swaps.append(send(a, outs[a].at[place], place, other))
        for k, a in steps:
            late[k, a].wait_recv()
            place = slot(1 - x, (z - k + zs) % zs, 1 - y, c)
            swaps.append(send(a, outs[a].at[place], place, other))
        for copy in swaps:
            copy.wait_recv()
        for copy in sent:
            copy.wait_send()
        return

    def across(places, targets):
        for place in places:
            for a in range(count):
                for target in targets:
                    send(a, outs[a].at[place], place, target)

    def settle():
        for copy in sent:
            copy.wait()
        del sent[:]

    settle()
    across(
        [slot(x, zz, y, c) for zz in range(zs)],
        [device(x, z, (y + k) % ys, c) for k in range(1, ys)],
    )
    settle()
    across(
        [slot(x, zz, yy, c) for zz in range(zs) for yy in range(ys)],
        [device((x + k) % xs, z, y, c) for k in range(1, xs)],
    )
    settle()
    across(
        [slot(xx, zz, yy, c) for xx in range(xs) for zz in range(zs) for yy in range(ys)],
        [other],
    )
    settle()


def gather_kernel(dims, *refs):
    in_ref, out_ref, send_sem, recv_sem, local_sem = refs
    partners = gather_partners(dims)
    barrier = pltpu.get_barrier_semaphore()
    for partner in partners:
        pl.semaphore_signal(barrier, inc=1, device_id=partner, device_id_type=MESH)
    pl.semaphore_wait(barrier, len(partners))
    gather(dims, [in_ref], [out_ref], send_sem, recv_sem, local_sem)


def all_gather(dims, collective_id, slab):
    devices = dims[0] * dims[1] * dims[2] * dims[3]
    return pl.pallas_call(
        functools.partial(gather_kernel, dims),
        out_shape=jax.ShapeDtypeStruct((devices,) + slab.shape, slab.dtype),
        in_specs=[VMEM_SPEC],
        out_specs=VMEM_SPEC,
        scratch_shapes=[
            pltpu.SemaphoreType.DMA((devices - 1,)),
            pltpu.SemaphoreType.DMA((devices - 1,)),
            pltpu.SemaphoreType.DMA((1,)),
        ],
        compiler_params=pltpu.CompilerParams(collective_id=collective_id, has_side_effects=True),
    )(slab)


def split_rows(values):
    high = values.astype(jnp.bfloat16)
    low = (values - high.astype(jnp.float32)).astype(jnp.bfloat16)
    return jnp.concatenate([high, low], axis=0)


def solve_kernel(
    dims, groups,
    near_ref, valid_ref, side_ref, points_ref, own_points_ref, noise_ref, right_ref, guess_ref,
    field_out, residual_out,
    buffers, dir_ref, vectors_ref, blocks, outgoing, dot_ref, dots_ref,
    send_sem, recv_sem, local_sem, dot_send, dot_recv,
):
    cols = dims[1] * dims[2] * dims[3]
    devices = dims[0] * cols
    tiles, tile = points_ref.shape[0], points_ref.shape[2]
    own, rhs, _ = right_ref.shape
    me = lax.axis_index("row") * cols + lax.axis_index("col")

    def peer(k):
        number = (me + k) % devices
        return (number // cols, number % cols)

    barrier = pltpu.get_barrier_semaphore()

    def greet(k, carry):
        pl.semaphore_signal(barrier, inc=1, device_id=peer(k), device_id_type=MESH)
        return carry

    lax.fori_loop(1, devices, greet, 0)
    pl.semaphore_wait(barrier, devices - 1)

    def spread(number, source):
        gather(
            dims, [source], [buffers.at[number]],
            send_sem.at[number], recv_sem.at[number], local_sem.at[number],
        )

    rows = 32
    block = 2 * tile

    def build(e, carry):
        left = points_ref[near_ref[e]].T
        right = own_points_ref[side_ref[e // GROUP]]
        reach = valid_ref[e].astype(jnp.float32)
        for chunk in range(tile // rows):
            squared = None
            for component in range(3):
                spacing = (
                    left[chunk * rows : (chunk + 1) * rows, component : component + 1]
                    - right[component : component + 1, :]
                )
                term = spacing * spacing
                squared = term if squared is None else squared + term
            distance = squared * lax.rsqrt(jnp.maximum(squared, 1e-30))
            remain = jnp.maximum(reach - distance, 0.0)
            remain = remain * remain
            weights = remain * remain * (4.0 * distance + 1.0)
            high = weights.astype(jnp.bfloat16)
            low = (weights - high.astype(jnp.float32)).astype(jnp.bfloat16)
            at = pl.multiple_of(e * block + chunk * rows, rows)
            blocks[pl.ds(at, rows), :] = high
            at = pl.multiple_of(e * block + tile + chunk * rows, rows)
            blocks[pl.ds(at, rows), :] = low
        return carry

    def image_of():
        def step(g, totals):
            parts = []
            for i in range(GROUP):
                part = vectors_ref[near_ref[g * GROUP + i]]
                parts += [part, part]
            first = pl.multiple_of(g * GROUP * block, GROUP * block)
            term = jnp.dot(
                jnp.concatenate(parts, axis=1),
                blocks[pl.ds(first, GROUP * block), :],
                preferred_element_type=jnp.float32,
            )
            place = side_ref[g].astype(jnp.float32)
            return tuple(
                total + term * jnp.maximum(1.0 - jnp.abs(place - float(p)), 0.0)
                for p, total in enumerate(totals)
            )

        start = tuple(jnp.zeros((2 * rhs, tile), jnp.float32) for _ in range(own))
        totals = lax.fori_loop(0, groups, step, start, unroll=2)
        return [total[:rhs] + total[rhs:] for total in totals]

    def over_tiles(body, start):
        def one(i, carry):
            return body(i // own, i % own, carry)

        return lax.fori_loop(0, tiles, one, start, unroll=8)

    zero = jnp.zeros((rhs, tile), jnp.float32)
    noise = [noise_ref[p : p + 1, :] for p in range(own)]

    lax.fori_loop(0, groups * GROUP, build, 0)
    spread(0, guess_ref)

    def take_guess(i, p, carry):
        vectors_ref[i * own + p] = split_rows(buffers[0, i, p])
        return carry

    over_tiles(take_guess, 0)
    for p, image in enumerate(image_of()):
        outgoing[0, p] = right_ref[p] - (image + noise[p] * guess_ref[p])
    spread(1, outgoing.at[0])

    def take_residual(i, p, total):
        value = buffers[1, i, p]
        dir_ref[i, p] = value
        vectors_ref[i * own + p] = split_rows(value)
        return total + value * value

    norm = jnp.sum(over_tiles(take_residual, zero), axis=1, keepdims=True)
    for p in range(own):
        field_out[p] = guess_ref[p]
    for iteration in range(1, ITERS):
        for p, image in enumerate(image_of()):
            outgoing[iteration, p] = image + noise[p] * dir_ref[me, p]
        spread(1 + iteration, outgoing.at[iteration])

        def dots(i, p, total):
            return total + dir_ref[i, p] * buffers[1 + iteration, i, p]

        inner = jnp.sum(over_tiles(dots, zero), axis=1, keepdims=True)
        step_size = norm / inner
        for p in range(own):
            field_out[p] = field_out[p] + step_size * dir_ref[me, p]

        def descend(i, p, total):
            value = buffers[1, i, p] - step_size * buffers[1 + iteration, i, p]
            buffers[1, i, p] = value
            return total + value * value

        norm_next = jnp.sum(over_tiles(descend, zero), axis=1, keepdims=True)
        turn = norm_next / norm

        def redirect(i, p, carry):
            value = buffers[1, i, p] + turn * dir_ref[i, p]
            dir_ref[i, p] = value
            vectors_ref[i * own + p] = split_rows(value)
            return carry

        over_tiles(redirect, 0)
        norm = norm_next

    images, total = [], zero
    for p, image in enumerate(image_of()):
        value = dir_ref[me, p]
        image = image + noise[p] * value
        images.append(image)
        total = total + value * image
    eye = lax.broadcasted_iota(jnp.int32, (rhs, 128), 0) == lax.broadcasted_iota(
        jnp.int32, (rhs, 128), 1
    )
    share = jnp.sum(total, axis=1, keepdims=True)
    row = jnp.sum(jnp.where(eye, share, 0.0), axis=0, keepdims=True)
    dot_ref[...] = row
    dots_ref[me] = row

    def dot_copy(k):
        return pltpu.make_async_remote_copy(
            src_ref=dot_ref,
            dst_ref=dots_ref.at[me],
            send_sem=dot_send.at[k],
            recv_sem=dot_recv.at[k],
            device_id=peer(k),
            device_id_type=MESH,
        )

    def start_dot(k, carry):
        dot_copy(k).start()
        return carry

    def wait_dot(k, carry):
        dot_copy(k).wait()
        return carry

    lax.fori_loop(1, devices, start_dot, 0)
    lax.fori_loop(1, devices, wait_dot, 0)
    inner = jnp.sum(dots_ref[...], axis=0)
    inner = jnp.sum(jnp.where(eye, inner, 0.0), axis=1, keepdims=True)
    step_size = norm / inner
    for p in range(own):
        field_out[p] = field_out[p] + step_size * dir_ref[me, p]
        residual_out[p] = buffers[1, me, p] - step_size * images[p]


def solve(dims, groups, collective_id, *operands):
    devices = dims[0] * dims[1] * dims[2] * dims[3]
    points, right = operands[3], operands[6]
    tiles, tile = points.shape[0], points.shape[2]
    own, rhs, _ = right.shape
    dma = pltpu.SemaphoreType.DMA
    phases = 1 + ITERS
    return pl.pallas_call(
        functools.partial(solve_kernel, dims, groups),
        out_shape=[jax.ShapeDtypeStruct(right.shape, jnp.float32)] * 2,
        in_specs=[SMEM_SPEC] * 3 + [VMEM_SPEC] * 5,
        out_specs=[VMEM_SPEC] * 2,
        scratch_shapes=[
            pltpu.VMEM((phases, devices, own, rhs, tile), jnp.float32),
            pltpu.VMEM((devices, own, rhs, tile), jnp.float32),
            pltpu.VMEM((tiles, 2 * rhs, tile), jnp.bfloat16),
            pltpu.VMEM((groups * GROUP * 2 * tile, tile), jnp.bfloat16),
            pltpu.VMEM((ITERS, own, rhs, tile), jnp.float32),
            pltpu.VMEM((1, 128), jnp.float32),
            pltpu.VMEM((devices, 1, 128), jnp.float32),
            dma((phases, devices - 1)),
            dma((phases, devices - 1)),
            dma((phases, 1)),
            dma((devices,)),
            dma((devices,)),
        ],
        compiler_params=pltpu.CompilerParams(
            collective_id=collective_id, has_side_effects=True, vmem_limit_bytes=60 * 2**20
        ),
    )(*operands)


def shards(mesh_shape, coords, noise_var, right_side, start_guess, tile_pairs):
    dims = factors(mesh_shape)
    devices = mesh_shape[0] * mesh_shape[1]
    own, _, tile = coords.shape
    tiles = own * devices
    me = lax.axis_index("row") * mesh_shape[1] + lax.axis_index("col")
    padded = jnp.pad(coords, ((0, 0), (0, 5), (0, 0)))
    points = all_gather(dims, 0, padded).reshape(tiles, 8, tile)

    low, high = jnp.min(points, axis=2), jnp.max(points, axis=2)
    gap = jnp.maximum(low[None] - high[:, None], low[:, None] - high[None])
    near = jnp.all(gap < 1.0, axis=2).astype(jnp.int32)
    needed = -(-jnp.sum(near, axis=1) // GROUP)
    largest = jnp.max(jnp.sum(needed.reshape(devices, own), axis=1))
    own_near = lax.dynamic_slice_in_dim(near, me * own, own)
    own_needed = lax.dynamic_slice_in_dim(needed, me * own, own)
    ids = jnp.arange(tiles, dtype=jnp.int32)
    rank = jnp.sum(own_near[:, None, :] * (ids[None, None, :] < ids[None, :, None]), axis=2)
    places = jnp.arange(own, dtype=jnp.int32)
    first = jnp.sum(own_needed[None, :] * (places[None, :] < places[:, None]), axis=1)
    goal = jnp.where(own_near > 0, rank + first[:, None] * GROUP, -1)
    capacity = own * CAPACITY
    slots = jnp.arange(capacity, dtype=jnp.int32)
    hit = goal[None] == slots[:, None, None]
    near_ids = jnp.sum(jnp.where(hit, ids[None, None, :], 0), axis=(1, 2)).astype(jnp.int32)
    valid = jnp.sum(hit, axis=(1, 2)).astype(jnp.int32)
    group_ids = jnp.arange(capacity // GROUP, dtype=jnp.int32)
    side = jnp.sum(group_ids[:, None] >= first[None, 1:], axis=1).astype(jnp.int32)

    operands = (near_ids, valid, side, points, padded, noise_var, right_side, start_guess)
    small = own * 4
    return tuple(
        lax.cond(
            largest <= small,
            functools.partial(solve, dims, small, 1),
            functools.partial(solve, dims, capacity // GROUP, 2),
            *operands,
        )
    )


def solution(mesh):
    placed = (
        P(("row", "col"), None, None),
        P(("row", "col"), None),
        P(("row", "col"), None, None),
        P(("row", "col"), None, None),
        P("row", "col", None, None),
    )
    return jax.shard_map(
        functools.partial(shards, (mesh.shape["row"], mesh.shape["col"])),
        mesh=mesh,
        in_specs=placed,
        out_specs=(P(("row", "col"), None, None), P(("row", "col"), None, None)),
        check_vma=False,
    )
```

```python
import functools

import jax
import jax.numpy as jnp
from jax import lax
from jax.experimental import pallas as pl
from jax.experimental.pallas import tpu as pltpu
from jax.sharding import PartitionSpec as P

ITERS = 3
GROUP = 4
NEAR = 27
CAPACITY = -(-NEAR // GROUP) * GROUP
CORES = 2
MESH = pl.DeviceIdType.MESH
VMEM_SPEC = pl.BlockSpec(memory_space=pltpu.VMEM)
SMEM_SPEC = pl.BlockSpec(memory_space=pltpu.SMEM)
ANY_SPEC = pl.BlockSpec(memory_space=pl.ANY)


def factors(mesh_shape):
    rows, cols = mesh_shape
    chips = cols // CORES
    wide = 1
    while wide * wide * 4 <= chips:
        wide *= 2
    return rows, chips // wide, wide, CORES


def position(dims):
    xs, zs, ys, cs = dims
    x = lax.axis_index("row")
    col = lax.axis_index("col")
    return x, col // (ys * cs), (col // cs) % ys, col % cs


def gather_partners(dims):
    xs, zs, ys, cs = dims
    x, z, y, c = position(dims)
    partners = [(x, (((z + k) % zs) * ys + y) * cs + c) for k in range(1, zs)]
    partners += [(x, (z * ys + (y + k) % ys) * cs + c) for k in range(1, ys)]
    partners += [((x + k) % xs, (z * ys + y) * cs + c) for k in range(1, xs)]
    partners += [(x, (z * ys + y) * cs + 1 - c)]
    return partners


def gather(dims, ins, outs, send_sem, recv_sem, local_sem):
    xs, zs, ys, cs = dims
    count = len(ins)
    x, z, y, c = position(dims)

    def device(xx, zz, yy, cc):
        return (xx, (zz * ys + yy) * cs + cc)

    def slot(xx, zz, yy, cc):
        return ((xx * zs + zz) * ys + yy) * cs + cc

    local = []
    for a in range(count):
        copy = pltpu.make_async_copy(ins[a], outs[a].at[slot(x, z, y, c)], local_sem.at[a])
        copy.start()
        local.append(copy)

    numbers = iter(range(10**6))
    sent = []

    def send(a, source, place, target):
        number = next(numbers)
        copy = pltpu.make_async_remote_copy(
            src_ref=source,
            dst_ref=outs[a].at[place],
            send_sem=send_sem.at[number],
            recv_sem=recv_sem.at[number],
            device_id=target,
            device_id_type=MESH,
        )
        copy.start()
        sent.append(copy)
        return copy

    mine = slot(x, z, y, c)
    other = device(x, z, y, 1 - c)
    along_z = {}
    for k in range(1, zs):
        for a in range(count):
            along_z[k, a] = send(a, ins[a], mine, device(x, (z + k) % zs, y, c))
    yield
    for a in range(count):
        local[a].wait()

    if xs == 2 and ys == 2:
        x2, y2 = (x + c) % 2, (y + 1 - c) % 2
        x3, y3 = (x + 1 - c) % 2, (y + c) % 2
        ahead, aside, late, swaps = {}, {}, {}, []
        steps = [(k, a) for k in range(zs) for a in range(count)]
        for k, a in steps:
            if k:
                along_z[k, a].wait_recv()
            place = slot(x, (z - k + zs) % zs, y, c)
            ahead[k, a] = send(a, outs[a].at[place], place, device(x2, z, y2, c))
            aside[k, a] = send(a, outs[a].at[place], place, device(x3, z, y3, c))
            swaps.append(send(a, outs[a].at[place], place, other))
        yield
        for k, a in steps:
            ahead[k, a].wait_recv()
            place = slot(x2, (z - k + zs) % zs, y2, c)
            late[k, a] = send(a, outs[a].at[place], place, device(x3, z, y3, c))
            swaps.append(send(a, outs[a].at[place], place, other))
        yield
        for k, a in steps:
            aside[k, a].wait_recv()
            place = slot(x3, (z - k + zs) % zs, y3, c)
            swaps.append(send(a, outs[a].at[place], place, other))
        for k, a in steps:
            late[k, a].wait_recv()
            place = slot(1 - x, (z - k + zs) % zs, 1 - y, c)
            swaps.append(send(a, outs[a].at[place], place, other))
        for copy in swaps:
            copy.wait_recv()
        for copy in sent:
            copy.wait_send()
        return

    def across(places, targets):
        for place in places:
            for a in range(count):
                for target in targets:
                    send(a, outs[a].at[place], place, target)

    def settle():
        for copy in sent:
            copy.wait()
        del sent[:]

    settle()
    across(
        [slot(x, zz, y, c) for zz in range(zs)],
        [device(x, z, (y + k) % ys, c) for k in range(1, ys)],
    )
    settle()
    across(
        [slot(x, zz, yy, c) for zz in range(zs) for yy in range(ys)],
        [device((x + k) % xs, z, y, c) for k in range(1, xs)],
    )
    settle()
    across(
        [slot(xx, zz, yy, c) for xx in range(xs) for zz in range(zs) for yy in range(ys)],
        [other],
    )
    settle()


def gather_kernel(dims, *refs):
    in_ref, out_ref, send_sem, recv_sem, local_sem = refs
    partners = gather_partners(dims)
    barrier = pltpu.get_barrier_semaphore()
    for partner in partners:
        pl.semaphore_signal(barrier, inc=1, device_id=partner, device_id_type=MESH)
    pl.semaphore_wait(barrier, len(partners))
    for _ in gather(dims, [in_ref], [out_ref], send_sem, recv_sem, local_sem):
        pass


def all_gather(dims, collective_id, slab):
    devices = dims[0] * dims[1] * dims[2] * dims[3]
    return pl.pallas_call(
        functools.partial(gather_kernel, dims),
        out_shape=jax.ShapeDtypeStruct((devices,) + slab.shape, slab.dtype),
        in_specs=[VMEM_SPEC],
        out_specs=VMEM_SPEC,
        scratch_shapes=[
            pltpu.SemaphoreType.DMA((devices - 1,)),
            pltpu.SemaphoreType.DMA((devices - 1,)),
            pltpu.SemaphoreType.DMA((1,)),
        ],
        compiler_params=pltpu.CompilerParams(collective_id=collective_id, has_side_effects=True),
    )(slab)


def split_rows(values):
    high = values.astype(jnp.bfloat16)
    low = (values - high.astype(jnp.float32)).astype(jnp.bfloat16)
    return jnp.concatenate([high, low], axis=0)


def solve_kernel(
    dims, groups,
    near_ref, side_ref, points_ref, own_points_ref, noise_ref, right_ref, guess_ref,
    field_out, residual_out,
    buffers, dir_ref, vectors_ref, blocks, outgoing, dot_ref, dots_ref,
    send_sem, recv_sem, local_sem, dot_send, dot_recv,
):
    cols = dims[1] * dims[2] * dims[3]
    devices = dims[0] * cols
    tiles, tile = points_ref.shape[0], points_ref.shape[2]
    own, rhs, _ = right_ref.shape
    me = lax.axis_index("row") * cols + lax.axis_index("col")

    def peer(k):
        number = (me + k) % devices
        return (number // cols, number % cols)

    barrier = pltpu.get_barrier_semaphore()

    def greet(k, carry):
        pl.semaphore_signal(barrier, inc=1, device_id=peer(k), device_id_type=MESH)
        return carry

    lax.fori_loop(1, devices, greet, 0)

    def spreading(number, source):
        return gather(
            dims, [source], [buffers.at[number]],
            send_sem.at[number], recv_sem.at[number], local_sem.at[number],
        )

    def spread(number, source):
        for _ in spreading(number, source):
            pass

    rows = 32
    block = 2 * tile

    def build(e, carry):
        left = points_ref[jnp.maximum(near_ref[e], 0)].T
        right = own_points_ref[side_ref[e // GROUP]]
        reach = jnp.minimum(near_ref[e] + 1, 1).astype(jnp.float32)
        for chunk in range(tile // rows):
            squared = None
            for component in range(3):
                spacing = (
                    left[chunk * rows : (chunk + 1) * rows, component : component + 1]
                    - right[component : component + 1, :]
                )
                term = spacing * spacing
                squared = term if squared is None else squared + term
            distance = squared * lax.rsqrt(jnp.maximum(squared, 1e-30))
            remain = jnp.maximum(reach - distance, 0.0)
            remain = remain * remain
            weights = remain * remain * (4.0 * distance + 1.0)
            high = weights.astype(jnp.bfloat16)
            low = (weights - high.astype(jnp.float32)).astype(jnp.bfloat16)
            at = pl.multiple_of(e * block + chunk * rows, rows)
            blocks[pl.ds(at, rows), :] = high
            at = pl.multiple_of(e * block + tile + chunk * rows, rows)
            blocks[pl.ds(at, rows), :] = low
        return carry

    def image_of():
        def step(g, totals):
            parts = []
            for i in range(GROUP):
                part = vectors_ref[jnp.maximum(near_ref[g * GROUP + i], 0)]
                parts += [part, part]
            first = pl.multiple_of(g * GROUP * block, GROUP * block)
            term = jnp.dot(
                jnp.concatenate(parts, axis=1),
                blocks[pl.ds(first, GROUP * block), :],
                preferred_element_type=jnp.float32,
            )
            place = side_ref[g].astype(jnp.float32)
            return tuple(
                total + term * jnp.maximum(1.0 - jnp.abs(place - float(p)), 0.0)
                for p, total in enumerate(totals)
            )

        start = tuple(jnp.zeros((2 * rhs, tile), jnp.float32) for _ in range(own))
        totals = lax.fori_loop(0, groups, step, start, unroll=2)
        return [total[:rhs] + total[rhs:] for total in totals]

    def over_tiles(body, start):
        def one(i, carry):
            return body(i // own, i % own, carry)

        return lax.fori_loop(0, tiles, one, start, unroll=8)

    zero = jnp.zeros((rhs, tile), jnp.float32)
    noise = [noise_ref[p : p + 1, :] for p in range(own)]

    shares = 5
    bounds = [groups * GROUP * i // shares for i in range(shares + 1)]
    lax.fori_loop(bounds[0], bounds[1], build, 0)
    pl.semaphore_wait(barrier, devices - 1)
    built = 1
    for _ in spreading(0, guess_ref):
        lax.fori_loop(bounds[built], bounds[built + 1], build, 0)
        built += 1
    lax.fori_loop(bounds[built], bounds[shares], build, 0)

    def take_guess(i, p, carry):
        vectors_ref[i * own + p] = split_rows(buffers[0, i, p])
        return carry

    over_tiles(take_guess, 0)
    for p, image in enumerate(image_of()):
        outgoing[0, p] = right_ref[p] - (image + noise[p] * guess_ref[p])
    spread(1, outgoing.at[0])

    def take_residual(i, p, total):
        value = buffers[1, i, p]
        dir_ref[i, p] = value
        vectors_ref[i * own + p] = split_rows(value)
        return total + value * value

    norm = jnp.sum(over_tiles(take_residual, zero), axis=1, keepdims=True)
    for p in range(own):
        field_out[p] = guess_ref[p]
    for iteration in range(1, ITERS):
        for p, image in enumerate(image_of()):
            outgoing[iteration, p] = image + noise[p] * dir_ref[me, p]
        spread(1 + iteration, outgoing.at[iteration])

        def dots(i, p, total):
            return total + dir_ref[i, p] * buffers[1 + iteration, i, p]

        inner = jnp.sum(over_tiles(dots, zero), axis=1, keepdims=True)
        step_size = norm / inner
        for p in range(own):
            field_out[p] = field_out[p] + step_size * dir_ref[me, p]

        def descend(i, p, total):
            value = buffers[1, i, p] - step_size * buffers[1 + iteration, i, p]
            buffers[1, i, p] = value
            return total + value * value

        norm_next = jnp.sum(over_tiles(descend, zero), axis=1, keepdims=True)
        turn = norm_next / norm

        def redirect(i, p, carry):
            value = buffers[1, i, p] + turn * dir_ref[i, p]
            dir_ref[i, p] = value
            vectors_ref[i * own + p] = split_rows(value)
            return carry

        over_tiles(redirect, 0)
        norm = norm_next

    images, total = [], zero
    for p, image in enumerate(image_of()):
        value = dir_ref[me, p]
        image = image + noise[p] * value
        images.append(image)
        total = total + value * image
    eye = lax.broadcasted_iota(jnp.int32, (rhs, 128), 0) == lax.broadcasted_iota(
        jnp.int32, (rhs, 128), 1
    )
    share = jnp.sum(total, axis=1, keepdims=True)
    row = jnp.sum(jnp.where(eye, share, 0.0), axis=0, keepdims=True)
    dot_ref[...] = row
    dots_ref[me] = row

    def dot_copy(k):
        return pltpu.make_async_remote_copy(
            src_ref=dot_ref,
            dst_ref=dots_ref.at[me],
            send_sem=dot_send.at[k],
            recv_sem=dot_recv.at[k],
            device_id=peer(k),
            device_id_type=MESH,
        )

    def start_dot(k, carry):
        dot_copy(k).start()
        return carry

    def wait_dot(k, carry):
        dot_copy(k).wait()
        return carry

    lax.fori_loop(1, devices, start_dot, 0)
    lax.fori_loop(1, devices, wait_dot, 0)
    inner = jnp.sum(dots_ref[...], axis=0)
    inner = jnp.sum(jnp.where(eye, inner, 0.0), axis=1, keepdims=True)
    step_size = norm / inner
    for p in range(own):
        field_out[p] = field_out[p] + step_size * dir_ref[me, p]
        residual_out[p] = buffers[1, me, p] - step_size * images[p]


def solve(dims, groups, collective_id, *operands):
    devices = dims[0] * dims[1] * dims[2] * dims[3]
    points, right = operands[2], operands[5]
    tiles, tile = points.shape[0], points.shape[2]
    own, rhs, _ = right.shape
    dma = pltpu.SemaphoreType.DMA
    phases = 1 + ITERS
    return pl.pallas_call(
        functools.partial(solve_kernel, dims, groups),
        out_shape=[jax.ShapeDtypeStruct(right.shape, jnp.float32)] * 2,
        in_specs=[SMEM_SPEC] * 2 + [VMEM_SPEC] * 5,
        out_specs=[VMEM_SPEC] * 2,
        scratch_shapes=[
            pltpu.VMEM((phases, devices, own, rhs, tile), jnp.float32),
            pltpu.VMEM((devices, own, rhs, tile), jnp.float32),
            pltpu.VMEM((tiles, 2 * rhs, tile), jnp.bfloat16),
            pltpu.VMEM((groups * GROUP * 2 * tile, tile), jnp.bfloat16),
            pltpu.VMEM((ITERS, own, rhs, tile), jnp.float32),
            pltpu.VMEM((1, 128), jnp.float32),
            pltpu.VMEM((devices, 1, 128), jnp.float32),
            dma((phases, devices - 1)),
            dma((phases, devices - 1)),
            dma((phases, 1)),
            dma((devices,)),
            dma((devices,)),
        ],
        compiler_params=pltpu.CompilerParams(
            collective_id=collective_id, has_side_effects=True, vmem_limit_bytes=60 * 2**20
        ),
    )(*operands)


def shards(mesh_shape, coords, noise_var, right_side, start_guess, tile_pairs):
    dims = factors(mesh_shape)
    devices = mesh_shape[0] * mesh_shape[1]
    own, _, tile = coords.shape
    tiles = own * devices
    me = lax.axis_index("row") * mesh_shape[1] + lax.axis_index("col")
    padded = jnp.pad(coords, ((0, 0), (0, 5), (0, 0)))
    points = all_gather(dims, 0, padded).reshape(tiles, 8, tile)

    low, high = jnp.min(points, axis=2), jnp.max(points, axis=2)
    gap = jnp.maximum(low[None] - high[:, None], low[:, None] - high[None])
    near = jnp.all(gap < 1.0, axis=2).astype(jnp.int32)
    needed = -(-jnp.sum(near, axis=1) // GROUP)
    largest = jnp.max(jnp.sum(needed.reshape(devices, own), axis=1))
    own_near = lax.dynamic_slice_in_dim(near, me * own, own)
    own_needed = lax.dynamic_slice_in_dim(needed, me * own, own)
    ids = jnp.arange(tiles, dtype=jnp.int32)
    rank = jnp.sum(own_near[:, None, :] * (ids[None, None, :] < ids[None, :, None]), axis=2)
    places = jnp.arange(own, dtype=jnp.int32)
    first = jnp.sum(own_needed[None, :] * (places[None, :] < places[:, None]), axis=1)
    goal = jnp.where(own_near > 0, rank + first[:, None] * GROUP, -1)
    capacity = own * CAPACITY
    slots = jnp.arange(capacity, dtype=jnp.int32)
    hit = goal.reshape(1, own * tiles) == slots[:, None]
    known = jnp.tile(ids + 1, own)[None]
    near_ids = (jnp.sum(jnp.where(hit, known, 0), axis=1) - 1).astype(jnp.int32)
    group_ids = jnp.arange(capacity // GROUP, dtype=jnp.int32)
    side = jnp.sum(group_ids[:, None] >= first[None, 1:], axis=1).astype(jnp.int32)

    near_ids, side, largest = lax.optimization_barrier((near_ids, side, largest))
    operands = (near_ids, side, points, padded, noise_var, right_side, start_guess)
    small = own * 4
    return tuple(
        lax.cond(
            largest <= small,
            functools.partial(solve, dims, small, 1),
            functools.partial(solve, dims, capacity // GROUP, 2),
            *operands,
        )
    )


def solution(mesh):
    placed = (
        P(("row", "col"), None, None),
        P(("row", "col"), None),
        P(("row", "col"), None, None),
        P(("row", "col"), None, None),
        P("row", "col", None, None),
    )
    return jax.shard_map(
        functools.partial(shards, (mesh.shape["row"], mesh.shape["col"])),
        mesh=mesh,
        in_specs=placed,
        out_specs=(P(("row", "col"), None, None), P(("row", "col"), None, None)),
        check_vma=False,
    )
```

```python
import functools

import jax
import jax.numpy as jnp
from jax import lax
from jax.experimental import pallas as pl
from jax.experimental.pallas import tpu as pltpu
from jax.sharding import PartitionSpec as P

ITERS = 3
GROUP = 4
NEAR = 27
CAPACITY = -(-NEAR // GROUP) * GROUP
CORES = 2
MESH = pl.DeviceIdType.MESH
VMEM_SPEC = pl.BlockSpec(memory_space=pltpu.VMEM)
SMEM_SPEC = pl.BlockSpec(memory_space=pltpu.SMEM)
ANY_SPEC = pl.BlockSpec(memory_space=pl.ANY)


def factors(mesh_shape):
    rows, cols = mesh_shape
    chips = cols // CORES
    wide = 1
    while wide * wide * 4 <= chips:
        wide *= 2
    return rows, chips // wide, wide, CORES


def position(dims):
    xs, zs, ys, cs = dims
    x = lax.axis_index("row")
    col = lax.axis_index("col")
    return x, col // (ys * cs), (col // cs) % ys, col % cs


def flip(index, k, size):
    if size & (size - 1):
        return (k - index + 2 * size) % size
    result, bit = 0, 1
    while bit < size:
        result = result + (index // bit + k // bit) % 2 * bit
        bit *= 2
    return result


def gather_partners(dims):
    xs, zs, ys, cs = dims
    x, z, y, c = position(dims)
    partners = [(x, (((z + k) % zs) * ys + y) * cs + c) for k in range(1, zs)]
    if xs == 2 and ys == 2:
        partners += [(1 - x, (z * ys + 1 - y) * cs + c)]
    partners += [(x, (z * ys + (y + k) % ys) * cs + c) for k in range(1, ys)]
    partners += [((x + k) % xs, (z * ys + y) * cs + c) for k in range(1, xs)]
    partners += [(x, (z * ys + y) * cs + 1 - c)]
    return partners


def gather(dims, ins, outs, send_sem, recv_sem, local_sem):
    xs, zs, ys, cs = dims
    count = len(ins)
    x, z, y, c = position(dims)

    def device(xx, zz, yy, cc):
        return (xx, (zz * ys + yy) * cs + cc)

    def slot(xx, zz, yy, cc):
        return ((xx * zs + zz) * ys + yy) * cs + cc

    local = []
    for a in range(count):
        copy = pltpu.make_async_copy(ins[a], outs[a].at[slot(x, z, y, c)], local_sem.at[a])
        copy.start()
        local.append(copy)

    numbers = iter(range(10**6))
    sent = []

    def send(a, source, place, target):
        number = next(numbers)
        copy = pltpu.make_async_remote_copy(
            src_ref=source,
            dst_ref=outs[a].at[place],
            send_sem=send_sem.at[number],
            recv_sem=recv_sem.at[number],
            device_id=target,
            device_id_type=MESH,
        )
        copy.start()
        sent.append(copy)
        return copy

    mine = slot(x, z, y, c)
    other = device(x, z, y, 1 - c)
    along_z = {}
    for k in reversed(range(1, zs)):
        for a in range(count):
            along_z[k, a] = send(a, ins[a], mine, device(x, flip(z, k, zs), y, c))
    yield
    for a in range(count):
        local[a].wait()

    if xs == 2 and ys == 2:
        across_by = ((1 - x, 1 - y), ((x + c) % 2, (y + 1 - c) % 2), ((x + 1 - c) % 2, (y + c) % 2))
        arrivals, swaps = [], []
        for k in range(zs):
            level = flip(z, k, zs)
            for a in range(count):
                if k:
                    along_z[k, a].wait_recv()
                place = slot(x, level, y, c)
                for xx, yy in across_by:
                    copy = send(a, outs[a].at[place], place, device(xx, z, yy, c))
                    arrivals.append((copy, a, slot(xx, level, yy, c)))
                swaps.append(send(a, outs[a].at[place], place, other))
        yield
        for number, way in enumerate((1, 2, 0)):
            for copy, a, place in arrivals[way::3]:
                copy.wait_recv()
                swaps.append(send(a, outs[a].at[place], place, other))
            if number == 1:
                yield
        for copy in swaps:
            copy.wait_recv()
        for copy in sent:
            copy.wait_send()
        return

    def across(places, targets):
        for place in places:
            for a in range(count):
                for target in targets:
                    send(a, outs[a].at[place], place, target)

    def settle():
        for copy in sent:
            copy.wait()
        del sent[:]

    settle()
    across(
        [slot(x, zz, y, c) for zz in range(zs)],
        [device(x, z, (y + k) % ys, c) for k in range(1, ys)],
    )
    settle()
    across(
        [slot(x, zz, yy, c) for zz in range(zs) for yy in range(ys)],
        [device((x + k) % xs, z, y, c) for k in range(1, xs)],
    )
    settle()
    across(
        [slot(xx, zz, yy, c) for xx in range(xs) for zz in range(zs) for yy in range(ys)],
        [other],
    )
    settle()


def gather_kernel(dims, *refs):
    in_ref, out_ref, send_sem, recv_sem, local_sem = refs
    partners = gather_partners(dims)
    barrier = pltpu.get_barrier_semaphore()
    for partner in partners:
        pl.semaphore_signal(barrier, inc=1, device_id=partner, device_id_type=MESH)
    pl.semaphore_wait(barrier, len(partners))
    for _ in gather(dims, [in_ref], [out_ref], send_sem, recv_sem, local_sem):
        pass


def all_gather(dims, collective_id, slab):
    devices = dims[0] * dims[1] * dims[2] * dims[3]
    return pl.pallas_call(
        functools.partial(gather_kernel, dims),
        out_shape=jax.ShapeDtypeStruct((devices,) + slab.shape, slab.dtype),
        in_specs=[VMEM_SPEC],
        out_specs=VMEM_SPEC,
        scratch_shapes=[
            pltpu.SemaphoreType.DMA((devices - 1,)),
            pltpu.SemaphoreType.DMA((devices - 1,)),
            pltpu.SemaphoreType.DMA((1,)),
        ],
        compiler_params=pltpu.CompilerParams(collective_id=collective_id, has_side_effects=True),
    )(slab)


def split_rows(values):
    high = values.astype(jnp.bfloat16)
    low = (values - high.astype(jnp.float32)).astype(jnp.bfloat16)
    return jnp.concatenate([high, low], axis=0)


def solve_kernel(
    dims, groups,
    near_ref, side_ref, points_ref, own_points_ref, noise_ref, right_ref, guess_ref,
    field_out, residual_out,
    buffers, dir_ref, vectors_ref, blocks, outgoing, dot_ref, dots_ref,
    send_sem, recv_sem, local_sem, dot_send, dot_recv,
):
    cols = dims[1] * dims[2] * dims[3]
    devices = dims[0] * cols
    tiles, tile = points_ref.shape[0], points_ref.shape[2]
    own, rhs, _ = right_ref.shape
    me = lax.axis_index("row") * cols + lax.axis_index("col")

    def peer(k):
        number = (me + k) % devices
        return (number // cols, number % cols)

    barrier = pltpu.get_barrier_semaphore()

    def greet(k, carry):
        pl.semaphore_signal(barrier, inc=1, device_id=peer(k), device_id_type=MESH)
        return carry

    lax.fori_loop(1, devices, greet, 0)

    def spreading(number, source):
        return gather(
            dims, [source], [buffers.at[number]],
            send_sem.at[number], recv_sem.at[number], local_sem.at[number],
        )

    def spread(number, source):
        for _ in spreading(number, source):
            pass

    rows = 32
    block = 2 * tile

    def build(e, carry):
        left = points_ref[jnp.maximum(near_ref[e], 0)].T
        right = own_points_ref[side_ref[e // GROUP]]
        reach = jnp.minimum(near_ref[e] + 1, 1).astype(jnp.float32)
        for chunk in range(tile // rows):
            squared = None
            for component in range(3):
                spacing = (
                    left[chunk * rows : (chunk + 1) * rows, component : component + 1]
                    - right[component : component + 1, :]
                )
                term = spacing * spacing
                squared = term if squared is None else squared + term
            distance = squared * lax.rsqrt(jnp.maximum(squared, 1e-30))
            remain = jnp.maximum(reach - distance, 0.0)
            remain = remain * remain
            weights = remain * remain * (4.0 * distance + 1.0)
            high = weights.astype(jnp.bfloat16)
            low = (weights - high.astype(jnp.float32)).astype(jnp.bfloat16)
            at = pl.multiple_of(e * block + chunk * rows, rows)
            blocks[pl.ds(at, rows), :] = high
            at = pl.multiple_of(e * block + tile + chunk * rows, rows)
            blocks[pl.ds(at, rows), :] = low
        return carry

    def image_of():
        def step(g, totals):
            parts = []
            for i in range(GROUP):
                part = vectors_ref[jnp.maximum(near_ref[g * GROUP + i], 0)]
                parts += [part, part]
            first = pl.multiple_of(g * GROUP * block, GROUP * block)
            term = jnp.dot(
                jnp.concatenate(parts, axis=1),
                blocks[pl.ds(first, GROUP * block), :],
                preferred_element_type=jnp.float32,
            )
            place = side_ref[g].astype(jnp.float32)
            return tuple(
                total + term * jnp.maximum(1.0 - jnp.abs(place - float(p)), 0.0)
                for p, total in enumerate(totals)
            )

        start = tuple(jnp.zeros((2 * rhs, tile), jnp.float32) for _ in range(own))
        totals = lax.fori_loop(0, groups, step, start, unroll=2)
        return [total[:rhs] + total[rhs:] for total in totals]

    def over_tiles(body, start):
        def one(i, carry):
            return body(i // own, i % own, carry)

        return lax.fori_loop(0, tiles, one, start, unroll=16)

    zero = jnp.zeros((rhs, tile), jnp.float32)
    noise = [noise_ref[p : p + 1, :] for p in range(own)]

    shares = 5
    bounds = [groups * GROUP * i // shares for i in range(shares + 1)]
    lax.fori_loop(bounds[0], bounds[1], build, 0)
    pl.semaphore_wait(barrier, devices - 1)
    built = 1
    for _ in spreading(0, guess_ref):
        lax.fori_loop(bounds[built], bounds[built + 1], build, 0)
        built += 1
    lax.fori_loop(bounds[built], bounds[shares], build, 0)

    def take_guess(i, p, carry):
        vectors_ref[i * own + p] = split_rows(buffers[0, i, p])
        return carry

    over_tiles(take_guess, 0)
    for p, image in enumerate(image_of()):
        outgoing[0, p] = right_ref[p] - (image + noise[p] * guess_ref[p])
    spread(1, outgoing.at[0])

    def take_residual(i, p, total):
        value = buffers[1, i, p]
        dir_ref[i, p] = value
        vectors_ref[i * own + p] = split_rows(value)
        return total + value * value

    norm = jnp.sum(over_tiles(take_residual, zero), axis=1, keepdims=True)
    for p in range(own):
        field_out[p] = guess_ref[p]
    for iteration in range(1, ITERS):
        for p, image in enumerate(image_of()):
            outgoing[iteration, p] = image + noise[p] * dir_ref[me, p]
        spread(1 + iteration, outgoing.at[iteration])

        def dots(i, p, total):
            return total + dir_ref[i, p] * buffers[1 + iteration, i, p]

        inner = jnp.sum(over_tiles(dots, zero), axis=1, keepdims=True)
        step_size = norm / inner
        for p in range(own):
            field_out[p] = field_out[p] + step_size * dir_ref[me, p]

        def descend(i, p, total):
            value = buffers[1, i, p] - step_size * buffers[1 + iteration, i, p]
            buffers[1, i, p] = value
            return total + value * value

        norm_next = jnp.sum(over_tiles(descend, zero), axis=1, keepdims=True)
        turn = norm_next / norm

        def redirect(i, p, carry):
            value = buffers[1, i, p] + turn * dir_ref[i, p]
            dir_ref[i, p] = value
            vectors_ref[i * own + p] = split_rows(value)
            return carry

        over_tiles(redirect, 0)
        norm = norm_next

    images, total = [], zero
    for p, image in enumerate(image_of()):
        value = dir_ref[me, p]
        image = image + noise[p] * value
        images.append(image)
        total = total + value * image
    eye = lax.broadcasted_iota(jnp.int32, (rhs, 128), 0) == lax.broadcasted_iota(
        jnp.int32, (rhs, 128), 1
    )
    share = jnp.sum(total, axis=1, keepdims=True)
    row = jnp.sum(jnp.where(eye, share, 0.0), axis=0, keepdims=True)
    dot_ref[...] = row
    dots_ref[me] = row

    def dot_copy(k):
        return pltpu.make_async_remote_copy(
            src_ref=dot_ref,
            dst_ref=dots_ref.at[me],
            send_sem=dot_send.at[k],
            recv_sem=dot_recv.at[k],
            device_id=peer(k),
            device_id_type=MESH,
        )

    def start_dot(k, carry):
        dot_copy(k).start()
        return carry

    def wait_dot(k, carry):
        dot_copy(k).wait()
        return carry

    lax.fori_loop(1, devices, start_dot, 0)
    lax.fori_loop(1, devices, wait_dot, 0)
    inner = jnp.sum(dots_ref[...], axis=0)
    inner = jnp.sum(jnp.where(eye, inner, 0.0), axis=1, keepdims=True)
    step_size = norm / inner
    for p in range(own):
        field_out[p] = field_out[p] + step_size * dir_ref[me, p]
        residual_out[p] = buffers[1, me, p] - step_size * images[p]


def solve(dims, groups, collective_id, *operands):
    devices = dims[0] * dims[1] * dims[2] * dims[3]
    points, right = operands[2], operands[5]
    tiles, tile = points.shape[0], points.shape[2]
    own, rhs, _ = right.shape
    dma = pltpu.SemaphoreType.DMA
    phases = 1 + ITERS
    return pl.pallas_call(
        functools.partial(solve_kernel, dims, groups),
        out_shape=[jax.ShapeDtypeStruct(right.shape, jnp.float32)] * 2,
        in_specs=[SMEM_SPEC] * 2 + [VMEM_SPEC] * 5,
        out_specs=[VMEM_SPEC] * 2,
        scratch_shapes=[
            pltpu.VMEM((phases, devices, own, rhs, tile), jnp.float32),
            pltpu.VMEM((devices, own, rhs, tile), jnp.float32),
            pltpu.VMEM((tiles, 2 * rhs, tile), jnp.bfloat16),
            pltpu.VMEM((groups * GROUP * 2 * tile, tile), jnp.bfloat16),
            pltpu.VMEM((ITERS, own, rhs, tile), jnp.float32),
            pltpu.VMEM((1, 128), jnp.float32),
            pltpu.VMEM((devices, 1, 128), jnp.float32),
            dma((phases, devices - 1)),
            dma((phases, devices - 1)),
            dma((phases, 1)),
            dma((devices,)),
            dma((devices,)),
        ],
        compiler_params=pltpu.CompilerParams(
            collective_id=collective_id, has_side_effects=True, vmem_limit_bytes=60 * 2**20
        ),
    )(*operands)


def shards(mesh_shape, coords, noise_var, right_side, start_guess, tile_pairs):
    dims = factors(mesh_shape)
    devices = mesh_shape[0] * mesh_shape[1]
    own, _, tile = coords.shape
    tiles = own * devices
    me = lax.axis_index("row") * mesh_shape[1] + lax.axis_index("col")
    padded = jnp.pad(coords, ((0, 0), (0, 5), (0, 0)))
    points = all_gather(dims, 0, padded).reshape(tiles, 8, tile)

    low, high = jnp.min(points, axis=2), jnp.max(points, axis=2)
    gap = jnp.maximum(low[None] - high[:, None], low[:, None] - high[None])
    near = jnp.all(gap < 1.0, axis=2).astype(jnp.int32)
    needed = -(-jnp.sum(near, axis=1) // GROUP)
    largest = jnp.max(jnp.sum(needed.reshape(devices, own), axis=1))
    own_near = lax.dynamic_slice_in_dim(near, me * own, own)
    own_needed = lax.dynamic_slice_in_dim(needed, me * own, own)
    ids = jnp.arange(tiles, dtype=jnp.int32)
    rank = jnp.sum(own_near[:, None, :] * (ids[None, None, :] < ids[None, :, None]), axis=2)
    places = jnp.arange(own, dtype=jnp.int32)
    first = jnp.sum(own_needed[None, :] * (places[None, :] < places[:, None]), axis=1)
    goal = jnp.where(own_near > 0, rank + first[:, None] * GROUP, -1)
    capacity = own * CAPACITY
    slots = jnp.arange(capacity, dtype=jnp.int32)
    hit = goal.reshape(1, own * tiles) == slots[:, None]
    known = jnp.tile(ids + 1, own)[None]
    near_ids = (jnp.sum(jnp.where(hit, known, 0), axis=1) - 1).astype(jnp.int32)
    group_ids = jnp.arange(capacity // GROUP, dtype=jnp.int32)
    side = jnp.sum(group_ids[:, None] >= first[None, 1:], axis=1).astype(jnp.int32)

    near_ids, side, largest = lax.optimization_barrier((near_ids, side, largest))
    operands = (near_ids, side, points, padded, noise_var, right_side, start_guess)
    small = own * 4
    return tuple(
        lax.cond(
            largest <= small,
            functools.partial(solve, dims, small, 1),
            functools.partial(solve, dims, capacity // GROUP, 2),
            *operands,
        )
    )


def solution(mesh):
    placed = (
        P(("row", "col"), None, None),
        P(("row", "col"), None),
        P(("row", "col"), None, None),
        P(("row", "col"), None, None),
        P("row", "col", None, None),
    )
    return jax.shard_map(
        functools.partial(shards, (mesh.shape["row"], mesh.shape["col"])),
        mesh=mesh,
        in_specs=placed,
        out_specs=(P(("row", "col"), None, None), P(("row", "col"), None, None)),
        check_vma=False,
    )
```

```python
import functools

import jax
import jax.numpy as jnp
from jax import lax
from jax.experimental import pallas as pl
from jax.experimental.pallas import tpu as pltpu
from jax.sharding import PartitionSpec as P

ITERS = 3
GROUP = 4
NEAR = 27
CAPACITY = -(-NEAR // GROUP) * GROUP
CORES = 2
MESH = pl.DeviceIdType.MESH
VMEM_SPEC = pl.BlockSpec(memory_space=pltpu.VMEM)
SMEM_SPEC = pl.BlockSpec(memory_space=pltpu.SMEM)
ANY_SPEC = pl.BlockSpec(memory_space=pl.ANY)


def factors(mesh_shape):
    rows, cols = mesh_shape
    chips = cols // CORES
    wide = 1
    while wide * wide * 4 <= chips:
        wide *= 2
    return rows, chips // wide, wide, CORES


def position(dims):
    xs, zs, ys, cs = dims
    x = lax.axis_index("row")
    col = lax.axis_index("col")
    return x, col // (ys * cs), (col // cs) % ys, col % cs


def flip(index, k, size):
    if size & (size - 1):
        return (k - index + 2 * size) % size
    result, bit = 0, 1
    while bit < size:
        result = result + (index // bit + k // bit) % 2 * bit
        bit *= 2
    return result


def gather_partners(dims):
    xs, zs, ys, cs = dims
    x, z, y, c = position(dims)
    partners = [(x, (((z + k) % zs) * ys + y) * cs + c) for k in range(1, zs)]
    if xs == 2 and ys == 2:
        partners += [(1 - x, (z * ys + 1 - y) * cs + c)]
    partners += [(x, (z * ys + (y + k) % ys) * cs + c) for k in range(1, ys)]
    partners += [((x + k) % xs, (z * ys + y) * cs + c) for k in range(1, xs)]
    partners += [(x, (z * ys + y) * cs + 1 - c)]
    return partners


def gather(dims, ins, outs, send_sem, recv_sem, local_sem):
    xs, zs, ys, cs = dims
    count = len(ins)
    x, z, y, c = position(dims)

    def device(xx, zz, yy, cc):
        return (xx, (zz * ys + yy) * cs + cc)

    def slot(xx, zz, yy, cc):
        return ((xx * zs + zz) * ys + yy) * cs + cc

    local = []
    for a in range(count):
        copy = pltpu.make_async_copy(ins[a], outs[a].at[slot(x, z, y, c)], local_sem.at[a])
        copy.start()
        local.append(copy)

    numbers = iter(range(10**6))
    sent = []

    def send(a, source, place, target):
        number = next(numbers)
        copy = pltpu.make_async_remote_copy(
            src_ref=source,
            dst_ref=outs[a].at[place],
            send_sem=send_sem.at[number],
            recv_sem=recv_sem.at[number],
            device_id=target,
            device_id_type=MESH,
        )
        copy.start()
        sent.append(copy)
        return copy

    mine = slot(x, z, y, c)
    other = device(x, z, y, 1 - c)
    along_z = {}
    for k in reversed(range(1, zs)):
        for a in range(count):
            along_z[k, a] = send(a, ins[a], mine, device(x, flip(z, k, zs), y, c))
    yield
    for a in range(count):
        local[a].wait()

    if xs == 2 and ys == 2:
        across_by = ((1 - x, 1 - y), ((x + c) % 2, (y + 1 - c) % 2), ((x + 1 - c) % 2, (y + c) % 2))
        arrivals, swaps = [], []
        for k in range(zs):
            level = flip(z, k, zs)
            for a in range(count):
                if k:
                    along_z[k, a].wait_recv()
                place = slot(x, level, y, c)
                for xx, yy in across_by:
                    copy = send(a, outs[a].at[place], place, device(xx, z, yy, c))
                    arrivals.append((copy, a, slot(xx, level, yy, c)))
                swaps.append(send(a, outs[a].at[place], place, other))
        yield
        for number, way in enumerate((1, 2, 0)):
            for copy, a, place in arrivals[way::3]:
                copy.wait_recv()
                swaps.append(send(a, outs[a].at[place], place, other))
            if number == 1:
                yield
        for copy in swaps:
            copy.wait_recv()
        for copy in sent:
            copy.wait_send()
        return

    def across(places, targets):
        for place in places:
            for a in range(count):
                for target in targets:
                    send(a, outs[a].at[place], place, target)

    def settle():
        for copy in sent:
            copy.wait()
        del sent[:]

    settle()
    across(
        [slot(x, zz, y, c) for zz in range(zs)],
        [device(x, z, (y + k) % ys, c) for k in range(1, ys)],
    )
    settle()
    across(
        [slot(x, zz, yy, c) for zz in range(zs) for yy in range(ys)],
        [device((x + k) % xs, z, y, c) for k in range(1, xs)],
    )
    settle()
    across(
        [slot(xx, zz, yy, c) for xx in range(xs) for zz in range(zs) for yy in range(ys)],
        [other],
    )
    settle()


def gather_kernel(dims, *refs):
    in_ref, out_ref, send_sem, recv_sem, local_sem = refs
    partners = gather_partners(dims)
    barrier = pltpu.get_barrier_semaphore()
    for partner in partners:
        pl.semaphore_signal(barrier, inc=1, device_id=partner, device_id_type=MESH)
    pl.semaphore_wait(barrier, len(partners))
    for _ in gather(dims, [in_ref], [out_ref], send_sem, recv_sem, local_sem):
        pass


def all_gather(dims, collective_id, slab):
    devices = dims[0] * dims[1] * dims[2] * dims[3]
    return pl.pallas_call(
        functools.partial(gather_kernel, dims),
        out_shape=jax.ShapeDtypeStruct((devices,) + slab.shape, slab.dtype),
        in_specs=[VMEM_SPEC],
        out_specs=VMEM_SPEC,
        scratch_shapes=[
            pltpu.SemaphoreType.DMA((devices - 1,)),
            pltpu.SemaphoreType.DMA((devices - 1,)),
            pltpu.SemaphoreType.DMA((1,)),
        ],
        compiler_params=pltpu.CompilerParams(collective_id=collective_id, has_side_effects=True),
    )(slab)


def split_rows(values):
    high = values.astype(jnp.bfloat16)
    low = (values - high.astype(jnp.float32)).astype(jnp.bfloat16)
    return jnp.concatenate([high, low], axis=0)


def solve_kernel(
    dims, groups,
    near_ref, side_ref, points_ref, own_points_ref, noise_ref, right_ref, guess_ref,
    field_out, residual_out,
    buffers, dir_ref, vectors_ref, blocks, outgoing, dot_ref, dots_ref,
    send_sem, recv_sem, local_sem, dot_send, dot_recv,
):
    cols = dims[1] * dims[2] * dims[3]
    devices = dims[0] * cols
    tiles, tile = points_ref.shape[0], points_ref.shape[2]
    own, rhs, _ = right_ref.shape
    me = lax.axis_index("row") * cols + lax.axis_index("col")

    def peer(k):
        number = (me + k) % devices
        return (number // cols, number % cols)

    barrier = pltpu.get_barrier_semaphore()

    def greet(k, carry):
        pl.semaphore_signal(barrier, inc=1, device_id=peer(k), device_id_type=MESH)
        return carry

    lax.fori_loop(1, devices, greet, 0)

    def spreading(number, source):
        return gather(
            dims, [source], [buffers.at[number]],
            send_sem.at[number], recv_sem.at[number], local_sem.at[number],
        )

    def spread(number, source):
        for _ in spreading(number, source):
            pass

    rows = 32
    block = 2 * tile

    def build(e, carry):
        left = points_ref[jnp.maximum(near_ref[e], 0)].T
        right = own_points_ref[side_ref[e // GROUP]]
        reach = jnp.minimum(near_ref[e] + 1, 1).astype(jnp.float32)
        for chunk in range(tile // rows):
            squared = None
            for component in range(3):
                spacing = (
                    left[chunk * rows : (chunk + 1) * rows, component : component + 1]
                    - right[component : component + 1, :]
                )
                term = spacing * spacing
                squared = term if squared is None else squared + term
            distance = squared * lax.rsqrt(jnp.maximum(squared, 1e-30))
            remain = jnp.maximum(reach - distance, 0.0)
            remain = remain * remain
            weights = remain * remain * (4.0 * distance + 1.0)
            high = weights.astype(jnp.bfloat16)
            low = (weights - high.astype(jnp.float32)).astype(jnp.bfloat16)
            at = pl.multiple_of(e * block + chunk * rows, rows)
            blocks[pl.ds(at, rows), :] = high
            at = pl.multiple_of(e * block + tile + chunk * rows, rows)
            blocks[pl.ds(at, rows), :] = low
        return carry

    def image_of():
        def step(g, totals):
            parts = []
            for i in range(GROUP):
                part = vectors_ref[jnp.maximum(near_ref[g * GROUP + i], 0)]
                parts += [part, part]
            first = pl.multiple_of(g * GROUP * block, GROUP * block)
            term = jnp.dot(
                jnp.concatenate(parts, axis=1),
                blocks[pl.ds(first, GROUP * block), :],
                preferred_element_type=jnp.float32,
            )
            place = side_ref[g].astype(jnp.float32)
            return tuple(
                total + term * jnp.maximum(1.0 - jnp.abs(place - float(p)), 0.0)
                for p, total in enumerate(totals)
            )

        start = tuple(jnp.zeros((2 * rhs, tile), jnp.float32) for _ in range(own))
        totals = lax.fori_loop(0, groups, step, start, unroll=4 if groups % 4 == 0 else 2)
        return [total[:rhs] + total[rhs:] for total in totals]

    def over_tiles(body, start):
        def one(i, carry):
            return body(i // own, i % own, carry)

        return lax.fori_loop(0, tiles, one, start, unroll=16)

    zero = jnp.zeros((rhs, tile), jnp.float32)
    noise = [noise_ref[p : p + 1, :] for p in range(own)]

    shares = 5
    bounds = [groups * GROUP // 2 * i // shares * 2 for i in range(shares + 1)]
    lax.fori_loop(bounds[0], bounds[1], build, 0, unroll=2)
    pl.semaphore_wait(barrier, devices - 1)
    built = 1
    for _ in spreading(0, guess_ref):
        lax.fori_loop(bounds[built], bounds[built + 1], build, 0, unroll=2)
        built += 1
    lax.fori_loop(bounds[built], bounds[shares], build, 0, unroll=2)

    def take_guess(i, p, carry):
        vectors_ref[i * own + p] = split_rows(buffers[0, i, p])
        return carry

    over_tiles(take_guess, 0)
    for p, image in enumerate(image_of()):
        outgoing[0, p] = right_ref[p] - (image + noise[p] * guess_ref[p])
    spread(1, outgoing.at[0])

    def take_residual(i, p, total):
        value = buffers[1, i, p]
        dir_ref[i, p] = value
        vectors_ref[i * own + p] = split_rows(value)
        return total + value * value

    norm = jnp.sum(over_tiles(take_residual, zero), axis=1, keepdims=True)
    for p in range(own):
        field_out[p] = guess_ref[p]
    for iteration in range(1, ITERS):
        for p, image in enumerate(image_of()):
            outgoing[iteration, p] = image + noise[p] * dir_ref[me, p]
        spread(1 + iteration, outgoing.at[iteration])

        def dots(i, p, total):
            return total + dir_ref[i, p] * buffers[1 + iteration, i, p]

        inner = jnp.sum(over_tiles(dots, zero), axis=1, keepdims=True)
        step_size = norm / inner
        for p in range(own):
            field_out[p] = field_out[p] + step_size * dir_ref[me, p]

        def descend(i, p, total):
            value = buffers[1, i, p] - step_size * buffers[1 + iteration, i, p]
            buffers[1, i, p] = value
            return total + value * value

        norm_next = jnp.sum(over_tiles(descend, zero), axis=1, keepdims=True)
        turn = norm_next / norm

        def redirect(i, p, carry):
            value = buffers[1, i, p] + turn * dir_ref[i, p]
            dir_ref[i, p] = value
            vectors_ref[i * own + p] = split_rows(value)
            return carry

        over_tiles(redirect, 0)
        norm = norm_next

    images, total = [], zero
    for p, image in enumerate(image_of()):
        value = dir_ref[me, p]
        image = image + noise[p] * value
        images.append(image)
        total = total + value * image
    eye = lax.broadcasted_iota(jnp.int32, (rhs, 128), 0) == lax.broadcasted_iota(
        jnp.int32, (rhs, 128), 1
    )
    share = jnp.sum(total, axis=1, keepdims=True)
    row = jnp.sum(jnp.where(eye, share, 0.0), axis=0, keepdims=True)
    dot_ref[...] = row
    dots_ref[me] = row

    def dot_copy(k):
        return pltpu.make_async_remote_copy(
            src_ref=dot_ref,
            dst_ref=dots_ref.at[me],
            send_sem=dot_send.at[k],
            recv_sem=dot_recv.at[k],
            device_id=peer(k),
            device_id_type=MESH,
        )

    def start_dot(k, carry):
        dot_copy(k).start()
        return carry

    def wait_dot(k, carry):
        dot_copy(k).wait()
        return carry

    lax.fori_loop(1, devices, start_dot, 0)
    lax.fori_loop(1, devices, wait_dot, 0)
    inner = jnp.sum(dots_ref[...], axis=0)
    inner = jnp.sum(jnp.where(eye, inner, 0.0), axis=1, keepdims=True)
    step_size = norm / inner
    for p in range(own):
        field_out[p] = field_out[p] + step_size * dir_ref[me, p]
        residual_out[p] = buffers[1, me, p] - step_size * images[p]


def solve(dims, groups, collective_id, *operands):
    devices = dims[0] * dims[1] * dims[2] * dims[3]
    points, right = operands[2], operands[5]
    tiles, tile = points.shape[0], points.shape[2]
    own, rhs, _ = right.shape
    dma = pltpu.SemaphoreType.DMA
    phases = 1 + ITERS
    return pl.pallas_call(
        functools.partial(solve_kernel, dims, groups),
        out_shape=[jax.ShapeDtypeStruct(right.shape, jnp.float32)] * 2,
        in_specs=[SMEM_SPEC] * 2 + [VMEM_SPEC] * 5,
        out_specs=[VMEM_SPEC] * 2,
        scratch_shapes=[
            pltpu.VMEM((phases, devices, own, rhs, tile), jnp.float32),
            pltpu.VMEM((devices, own, rhs, tile), jnp.float32),
            pltpu.VMEM((tiles, 2 * rhs, tile), jnp.bfloat16),
            pltpu.VMEM((groups * GROUP * 2 * tile, tile), jnp.bfloat16),
            pltpu.VMEM((ITERS, own, rhs, tile), jnp.float32),
            pltpu.VMEM((1, 128), jnp.float32),
            pltpu.VMEM((devices, 1, 128), jnp.float32),
            dma((phases, devices - 1)),
            dma((phases, devices - 1)),
            dma((phases, 1)),
            dma((devices,)),
            dma((devices,)),
        ],
        compiler_params=pltpu.CompilerParams(
            collective_id=collective_id, has_side_effects=True, vmem_limit_bytes=60 * 2**20
        ),
    )(*operands)


def shards(mesh_shape, coords, noise_var, right_side, start_guess, tile_pairs):
    dims = factors(mesh_shape)
    devices = mesh_shape[0] * mesh_shape[1]
    own, _, tile = coords.shape
    tiles = own * devices
    me = lax.axis_index("row") * mesh_shape[1] + lax.axis_index("col")
    padded = jnp.pad(coords, ((0, 0), (0, 5), (0, 0)))
    points = all_gather(dims, 0, padded).reshape(tiles, 8, tile)

    low, high = jnp.min(points, axis=2), jnp.max(points, axis=2)
    gap = jnp.maximum(low[None] - high[:, None], low[:, None] - high[None])
    near = jnp.all(gap < 1.0, axis=2).astype(jnp.int32)
    needed = -(-jnp.sum(near, axis=1) // GROUP)
    largest = jnp.max(jnp.sum(needed.reshape(devices, own), axis=1))
    own_near = lax.dynamic_slice_in_dim(near, me * own, own)
    own_needed = lax.dynamic_slice_in_dim(needed, me * own, own)
    ids = jnp.arange(tiles, dtype=jnp.int32)
    rank = jnp.sum(own_near[:, None, :] * (ids[None, None, :] < ids[None, :, None]), axis=2)
    places = jnp.arange(own, dtype=jnp.int32)
    first = jnp.sum(own_needed[None, :] * (places[None, :] < places[:, None]), axis=1)
    goal = jnp.where(own_near > 0, rank + first[:, None] * GROUP, -1)
    capacity = own * CAPACITY
    slots = jnp.arange(capacity, dtype=jnp.int32)
    hit = goal.reshape(1, own * tiles) == slots[:, None]
    known = jnp.tile(ids + 1, own)[None]
    near_ids = (jnp.sum(jnp.where(hit, known, 0), axis=1) - 1).astype(jnp.int32)
    group_ids = jnp.arange(capacity // GROUP, dtype=jnp.int32)
    side = jnp.sum(group_ids[:, None] >= first[None, 1:], axis=1).astype(jnp.int32)

    near_ids, side, largest = lax.optimization_barrier((near_ids, side, largest))
    operands = (near_ids, side, points, padded, noise_var, right_side, start_guess)
    small = own * 4
    return tuple(
        lax.cond(
            largest <= small,
            functools.partial(solve, dims, small, 1),
            functools.partial(solve, dims, capacity // GROUP, 2),
            *operands,
        )
    )


def solution(mesh):
    placed = (
        P(("row", "col"), None, None),
        P(("row", "col"), None),
        P(("row", "col"), None, None),
        P(("row", "col"), None, None),
        P("row", "col", None, None),
    )
    return jax.shard_map(
        functools.partial(shards, (mesh.shape["row"], mesh.shape["col"])),
        mesh=mesh,
        in_specs=placed,
        out_specs=(P(("row", "col"), None, None), P(("row", "col"), None, None)),
        check_vma=False,
    )
```
